32 devices in a mesh: dp: 8 (over y, x, core), tensor: 4 (over z).
Axes of the slice: x: 2, y: 2, z: 4, core: 2. Of those that a mesh axis runs over, the one named last changes fastest.
Arguments:
- tokens: bfloat16 [8192, 2048], P(('dp', 'tensor')), may hold values from -6 to 6
- segments: int32 [8, 1024], P('dp'), may hold values from 0 to 7, never falling along the last dimension, each value on 1 to 256 neighbouring positions
- w_query: bfloat16 [2048, 2048], P('dp', 'tensor'), may hold values from -0.125 to 0.125
- w_key: bfloat16 [2048, 1024], P('dp', 'tensor'), may hold values from -0.125 to 0.125
- w_value: bfloat16 [2048, 1024], P('dp', 'tensor'), may hold values from -0.125 to 0.125
- w_out: bfloat16 [2048, 2048], P('tensor', 'dp'), may hold values from -0.75 to 0.75
- w_gate: bfloat16 [2048, 6144], P('dp', 'tensor'), may hold values from -0.125 to 0.125
- w_up: bfloat16 [2048, 6144], P('dp', 'tensor'), may hold values from -0.125 to 0.125
- w_down: bfloat16 [6144, 2048], P('tensor', 'dp'), may hold values from -0.078125 to 0.078125
- attn_gain: float32 [2048], replicated, may hold values from 0.5 to 1.5
- mlp_gain: float32 [2048], replicated, may hold values from 0.5 to 1.5
- query_gain: float32 [128], replicated, may hold values from 0.1 to 1.9
- key_gain: float32 [128], replicated, may hold values from 0.1 to 1.9
- cotangent: bfloat16 [8192, 2048], P(('dp', 'tensor')), may hold values from -6 to 6
Outputs:
- output: float32 [8192, 2048], P(('dp', 'tensor'))
- tokens_grad: float32 [8192, 2048], P(('dp', 'tensor'))
- w_query_grad: float32 [2048, 2048], P('dp', 'tensor')
- w_key_grad: float32 [2048, 1024], P('dp', 'tensor')
- w_value_grad: float32 [2048, 1024], P('dp', 'tensor')
- w_out_grad: float32 [2048, 2048], P('tensor', 'dp')
- w_gate_grad: float32 [2048, 6144], P('dp', 'tensor')
- w_up_grad: float32 [2048, 6144], P('dp', 'tensor')
- w_down_grad: float32 [6144, 2048], P('tensor', 'dp')
- attn_gain_grad: float32 [2048], replicated
- mlp_gain_grad: float32 [2048], replicated
- query_gain_grad: float32 [128], replicated
- key_gain_grad: float32 [128], replicated
The draws below stay inside these ranges and needn't reach their ends.
Inputs may be any that keep to these rules, and one draw needn't show every extreme that they name: `segments`: within each packed sequence the document numbers never fall; every document has 1 to 256 tokens, and one has exactly that many.
All inputs are finite; a program needn't handle non-finite values.
Results may differ from the reference program's by a relative error of at most 0.019.
Values may be sent and summed in bfloat16 or wider, within the bound.
No kernel may reach another device: no remote copies, remote signals or barrier semaphores. Data moves between devices by JAX's collectives and lax.ppermute only.
A program may use at most 192 MiB of HBM per device.

```python
import math
import jax
import jax.numpy as jnp
import numpy as np
from jax import lax

D = 2048
H = 16
KV = 8
HD = 128
FF = 6144
LEN = 1024
SEQS = 1
NSEQ = 8
TOKENS = 8192


def levels(stream_key, extent, pieces, low, high):
    def one(axis_at, blocks):
        heights = jax.random.uniform(jax.random.fold_in(jax.random.fold_in(stream_key, 6), axis_at), (blocks,), jnp.float32, low / len(pieces), high / len(pieces))
        return jnp.repeat(jnp.exp(heights), extent[axis_at] // blocks).reshape((-1,) + (1,) * (len(extent) - axis_at - 1))

    factor_of = one(*pieces[0])
    for cut in pieces[1:]:
        factor_of = factor_of * one(*cut)
    return factor_of


def split_up(count, total, reach, lean):
    loads = [(1 << 20) // math.isqrt(standing ** lean) + 1 for standing in range(2, count + 1)]
    spare, counts = total - reach - (count - 1), [1] * (count - 1)
    while spare > 0:
        free = [i for i in range(count - 1) if counts[i] < reach]
        whole, remaining = sum([loads[i] for i in free]), spare
        for i in free:
            addition = min(reach - counts[i], max(1, remaining * loads[i] // whole), spare)
            counts[i] = counts[i] + addition
            spare = spare - addition
    return np.array([reach] + counts)


def uneven_parts(stream_key, number_of, total, most, skew):
    if number_of == 2:
        one = jax.random.randint(stream_key, (), max(1, total - most), min(most, total - 1) + 1)
        return jnp.stack([one, total - one])
    sizes = jnp.asarray(split_up(number_of, total, most, skew), jnp.int32)
    twos = (number_of - 1) // 2
    source_of, sink = sizes[1:1 + 2 * twos:2], sizes[2:2 + 2 * twos:2]
    room = jnp.minimum(source_of - 1, most - sink)
    moved = jax.random.randint(jax.random.fold_in(stream_key, 1), (twos,), 0, 1 << 20) % (room + 1)
    sizes = sizes.at[1:1 + 2 * twos:2].set(source_of - moved).at[2:2 + 2 * twos:2].set(sink + moved)
    return sizes[jax.random.permutation(jax.random.fold_in(stream_key, 2), number_of)]


def scatter_about(key, dims, scale, reach, split=(), held_as=jnp.bfloat16):
    drawn = scale * jax.random.normal(key, dims, jnp.float32)
    if split:
        drawn = drawn * levels(key, dims, split, -0.22, 0.18)
    return jnp.clip(drawn, -reach, reach).astype(held_as)


def setup_inputs(seed: int = 0) -> dict:
    streams_of = jax.random.split(jax.random.key(seed), 15)
    return {
        "tokens": scatter_about(streams_of[0], (TOKENS, D), 1.0, 6.0, ((0, 32),)),
        "segments": jax.vmap(lambda own: jnp.searchsorted(jnp.cumsum(uneven_parts(own, 8, LEN, LEN // 4, 1)), jnp.arange(LEN), side="right"))(jax.random.split(streams_of[1], NSEQ)).reshape((NSEQ, LEN)).astype(jnp.int32),
        "w_query": scatter_about(streams_of[2], (D, H * HD), D ** -0.5, 0.125, ((0, 8), (1, 4))),
        "w_key": scatter_about(streams_of[3], (D, KV * HD), D ** -0.5, 0.125, ((0, 8), (1, 4))),
        "w_value": scatter_about(streams_of[4], (D, KV * HD), D ** -0.5, 0.125, ((0, 8), (1, 4))),
        "w_out": scatter_about(streams_of[5], (H * HD, D), (H * HD // 32) ** -0.5, 0.75, ((0, 4), (1, 8))),
        "w_gate": scatter_about(streams_of[6], (D, FF), D ** -0.5, 0.125, ((0, 8), (1, 4))),
        "w_up": scatter_about(streams_of[7], (D, FF), D ** -0.5, 0.125, ((0, 8), (1, 4))),
        "w_down": scatter_about(streams_of[8], (FF, D), FF ** -0.5, 0.078125, ((0, 4), (1, 8))),
        "attn_gain": jnp.clip(1.0 + 0.1 * jax.random.normal(streams_of[9], (D,), jnp.float32), 0.5, 1.5),
        "mlp_gain": jnp.clip(1.0 + 0.1 * jax.random.normal(streams_of[10], (D,), jnp.float32), 0.5, 1.5),
        "query_gain": jnp.clip(1.0 + 0.18 * jax.random.normal(streams_of[11], (HD,), jnp.float32), 0.1, 1.9),
        "key_gain": jnp.clip(1.0 + 0.18 * jax.random.normal(streams_of[12], (HD,), jnp.float32), 0.1, 1.9),
        "cotangent": scatter_about(streams_of[13], (TOKENS, D), 1.0, 6.0, ((0, 32),)),
    }


@jax.custom_vjp
def low(v):
    return lax.optimization_barrier(v.astype(jnp.bfloat16)).astype(jnp.float32)

@jax.custom_vjp
def low_back(v):
    return v

def low_keep(v):
    return (low(v), None)

def low_pass(kept, grad):
    return (grad,)

def back_keep(v):
    return (v, None)

def back_low(kept, grad):
    return (low(grad),)
low.defvjp(low_keep, low_pass)
low_back.defvjp(back_keep, back_low)
EPSILON = 1e-06
THETA_BASE = 1000000.0
NEG_FILL = -1e+30

def highest_dot(left, right):
    return jnp.dot(left, right, precision=lax.Precision.HIGHEST, preferred_element_type=jnp.float32)

def rms_norm(values, gain):
    return values * lax.rsqrt(lax.optimization_barrier(jnp.mean(values * values, axis=-1, keepdims=True)) + EPSILON) * gain

def positions(seg_rows):
    offsets = jnp.arange(seg_rows.shape[-1], dtype=jnp.int32)
    before = jnp.concatenate([seg_rows[:, :1] - 1, seg_rows[:, :-1]], axis=1)
    starts = jnp.where(seg_rows != before, offsets[None, :], 0)
    return offsets[None, :] - lax.cummax(starts, axis=1)

def rope_tables(places):
    halfway = HD // 2
    frequency = THETA_BASE ** (-(jnp.arange(halfway, dtype=jnp.float32) * (2.0 / HD)))
    angles = places.astype(jnp.float32)[..., None] * frequency
    angles = jnp.concatenate([angles, angles], axis=-1)
    return (jnp.cos(angles), jnp.sin(angles))

def rotate(values, cosine, sine):
    halfway = values.shape[-1] // 2
    turned = jnp.concatenate([-values[..., halfway:], values[..., :halfway]], axis=-1)
    return values * cosine + turned * sine

def block_forward(inputs, seg_rows, w_query, w_key, w_value, w_out, w_gate, w_up, w_down, attn_gain, mlp_gain, query_gain, key_gain):
    seq_count = seg_rows.shape[0]
    row_count = seq_count * LEN
    groups = H // KV
    cosine, sine = rope_tables(positions(seg_rows))
    normed_one = low(rms_norm(inputs, attn_gain))
    queries = low_back(highest_dot(normed_one, w_query)).reshape(seq_count, LEN, KV, groups, HD)
    keys_raw = low_back(highest_dot(normed_one, w_key)).reshape(seq_count, LEN, KV, HD)
    values_low = low(low_back(highest_dot(normed_one, w_value))).reshape(seq_count, LEN, KV, HD)
    query_heads = low(rotate(rms_norm(queries, query_gain), cosine[:, :, None, None, :], sine[:, :, None, None, :]) * HD ** (-0.5))
    key_heads = low(rotate(rms_norm(keys_raw, key_gain), cosine[:, :, None, :], sine[:, :, None, :]))
    scores = low_back(jnp.einsum('bqkgd,bskd->bkgqs', query_heads, key_heads, precision=lax.Precision.HIGHEST))
    offsets = jnp.arange(LEN, dtype=jnp.int32)
    allowed = (seg_rows[:, :, None] == seg_rows[:, None, :]) & (offsets[None, None, :] <= offsets[None, :, None])
    scores = jnp.where(allowed[:, None, None], scores, NEG_FILL)
    prob_low = low(jax.nn.softmax(scores, axis=-1))
    attended = jnp.einsum('bkgqs,bskd->bqkgd', prob_low, values_low, precision=lax.Precision.HIGHEST).reshape(row_count, H * HD)
    attn_low = low_back(low(attended))
    middle = inputs + low_back(highest_dot(attn_low, w_out))
    normed_two = low(rms_norm(middle, mlp_gain))
    gate_pre = low_back(highest_dot(normed_two, w_gate))
    up_pre = low_back(highest_dot(normed_two, w_up))
    hidden = low(jax.nn.silu(gate_pre) * up_pre)
    return middle + low_back(highest_dot(hidden, w_down))

def reference(tokens, segments, w_query, w_key, w_value, w_out, w_gate, w_up, w_down, attn_gain, mlp_gain, query_gain, key_gain, cotangent):
    params_all = (w_query.astype(jnp.float32), w_key.astype(jnp.float32), w_value.astype(jnp.float32), w_out.astype(jnp.float32), w_gate.astype(jnp.float32), w_up.astype(jnp.float32), w_down.astype(jnp.float32), attn_gain.astype(jnp.float32), mlp_gain.astype(jnp.float32), query_gain.astype(jnp.float32), key_gain.astype(jnp.float32))
    group_count = segments.shape[0] // SEQS
    span_rows = SEQS * LEN

    def one_group(running, number):
        seg_here = lax.dynamic_slice_in_dim(segments, number * SEQS, SEQS, 0)
        rows_here = lax.dynamic_slice_in_dim(tokens, number * span_rows, span_rows, 0).astype(jnp.float32)
        upstream = lax.dynamic_slice_in_dim(cotangent, number * span_rows, span_rows, 0).astype(jnp.float32)

        def forward(inputs, *params):
            return block_forward(inputs, seg_here, *params)
        result, pullback = jax.vjp(forward, rows_here, *params_all)
        grads = pullback(upstream)
        running = tuple((sofar + piece for sofar, piece in zip(running, grads[1:])))
        return (running, (result, grads[0]))
    initial = tuple((jnp.zeros_like(param) for param in params_all))
    sums_all, (results, input_grads) = lax.scan(one_group, initial, jnp.arange(group_count, dtype=jnp.int32))
    return (results.reshape(TOKENS, D), input_grads.reshape(TOKENS, D), sums_all[0], sums_all[1], sums_all[2], sums_all[3], sums_all[4], sums_all[5], sums_all[6], sums_all[7], sums_all[8], sums_all[9], sums_all[10])
```

```python
import jax
import jax.numpy as jnp
from jax import lax
from jax.experimental import pallas as pl
from jax.experimental.pallas import tpu as pltpu
from jax.sharding import PartitionSpec as P

H = 16
KV = 8
HD = 128
EPSILON = 1e-06
THETA_BASE = 1000000.0
NEG_FILL = -1e30
REACH = 256
HALF = 128

BF = jnp.bfloat16
F32 = jnp.float32


def product(left, right):
    return jnp.dot(left, right, preferred_element_type=F32)


def product_back(left, right):
    return lax.dot_general(left, right, (((1,), (1,)), ((), ())), preferred_element_type=F32)


def product_over(left, right):
    return lax.dot_general(left, right, (((0,), (0,)), ((), ())), preferred_element_type=F32)


def inverse_rms(values):
    return lax.rsqrt(jnp.mean(values * values, axis=-1, keepdims=True) + EPSILON)


def norm_back(values, inv, gain, grad):
    scaled = grad * gain
    return inv * scaled - values * (inv**3 * jnp.mean(scaled * values, axis=-1, keepdims=True))


def positions(seg_rows):
    offsets = jnp.arange(seg_rows.shape[-1], dtype=jnp.int32)
    before = jnp.concatenate([seg_rows[:, :1] - 1, seg_rows[:, :-1]], axis=1)
    starts = jnp.where(seg_rows != before, offsets[None, :], 0)
    return offsets[None, :] - lax.cummax(starts, axis=1)


def rope_tables(places):
    halfway = HD // 2
    frequency = THETA_BASE ** (-(jnp.arange(halfway, dtype=F32) * (2.0 / HD)))
    angles = places.astype(F32)[..., None] * frequency
    cosine, sine = jnp.cos(angles), jnp.sin(angles)
    return (
        jnp.concatenate([cosine, cosine], axis=-1),
        jnp.concatenate([-sine, sine], axis=-1),
    )


def row_sum(values):
    return jnp.sum(values, axis=0, keepdims=True)


def dot_across(left, right, left_dim, right_dim):
    return lax.dot_general(
        left, right, (((left_dim,), (right_dim,)), ((), ())), preferred_element_type=F32
    )


def window_mask(start_ref, block, sub, reach, rows):
    base = block * reach - reach + sub
    key = lax.broadcasted_iota(jnp.int32, (reach + rows, rows), 0)
    query = lax.broadcasted_iota(jnp.int32, (reach + rows, rows), 1)
    first = start_ref[:, sub : sub + rows] - base
    return (key >= first) & (key <= query + reach)


def attention_forward(qkv, start, cosine, sine, gains, kv_local):
    rows_all = qkv.shape[0]
    groups = H // KV
    heads = kv_local * groups
    reach, rows = REACH, HALF
    q_width, k_width = heads * HD, kv_local * HD
    block = lambda width: pl.BlockSpec((reach, width), lambda i: (i, 0))

    def kernel(
        qkv_ref, start_ref, cos_ref, sin_ref, gain_ref,
        q_ref, k_ref, v_ref, attn_ref, lse_ref, key_scr, value_scr,
    ):
        step = pl.program_id(0)

        @pl.when(step == 0)
        def _():
            key_scr[0:reach, :] = jnp.zeros((reach, k_width), BF)
            value_scr[0:reach, :] = jnp.zeros((reach, k_width), BF)

        @pl.when(step > 0)
        def _():
            key_scr[0:reach, :] = key_scr[reach : 2 * reach, :]
            value_scr[0:reach, :] = value_scr[reach : 2 * reach, :]

        cos, sin = cos_ref[...], sin_ref[...]

        def turned(at, gain):
            raw = qkv_ref[:, at : at + HD]
            normed = raw * inverse_rms(raw) * gain
            return normed * cos + pltpu.roll(normed, HD // 2, 1) * sin

        for head in range(heads):
            at = head * HD
            q_ref[:, at : at + HD] = (turned(at, gain_ref[0:1, :]) * HD ** (-0.5)).astype(BF)
        for head in range(kv_local):
            at = head * HD
            key = turned(q_width + at, gain_ref[1:2, :]).astype(BF)
            k_ref[:, at : at + HD] = key
            key_scr[reach : 2 * reach, at : at + HD] = key
            value = qkv_ref[:, q_width + k_width + at : q_width + k_width + at + HD].astype(BF)
            v_ref[:, at : at + HD] = value
            value_scr[reach : 2 * reach, at : at + HD] = value
        for sub in range(0, reach, rows):
            allowed = window_mask(start_ref, step, sub, reach, rows)
            for kv in range(kv_local):
                key = key_scr[sub : sub + reach + rows, kv * HD : (kv + 1) * HD]
                value = value_scr[sub : sub + reach + rows, kv * HD : (kv + 1) * HD]
                for head in range(kv * groups, (kv + 1) * groups):
                    query = q_ref[sub : sub + rows, head * HD : (head + 1) * HD]
                    scores = jnp.where(allowed, dot_across(key, query, 1, 1), NEG_FILL)
                    highest = jnp.max(scores, axis=0, keepdims=True)
                    shifted = jnp.exp(scores - highest)
                    totals = row_sum(shifted)
                    probs = (shifted * (1.0 / totals)).astype(BF)
                    attn_ref[sub : sub + rows, head * HD : (head + 1) * HD] = dot_across(
                        probs, value, 0, 0
                    ).astype(BF)
                    lse_ref[head : head + 1, sub : sub + rows] = highest + jnp.log(totals)

    return pl.pallas_call(
        kernel,
        grid=(rows_all // reach,),
        in_specs=[
            block(q_width + 2 * k_width),
            pl.BlockSpec((1, reach), lambda i: (0, i)),
            block(HD),
            block(HD),
            pl.BlockSpec((2, HD), lambda i: (0, 0)),
        ],
        out_specs=[
            block(q_width),
            block(k_width),
            block(k_width),
            block(q_width),
            pl.BlockSpec((heads, reach), lambda i: (0, i)),
        ],
        out_shape=[
            jax.ShapeDtypeStruct((rows_all, q_width), BF),
            jax.ShapeDtypeStruct((rows_all, k_width), BF),
            jax.ShapeDtypeStruct((rows_all, k_width), BF),
            jax.ShapeDtypeStruct((rows_all, q_width), BF),
            jax.ShapeDtypeStruct((heads, rows_all), F32),
        ],
        scratch_shapes=[
            pltpu.VMEM((2 * reach, k_width), BF),
            pltpu.VMEM((2 * reach, k_width), BF),
        ],
        name="attention_forward",
    )(qkv, start, cosine, sine, gains)


def attention_backward(
    qkv, start, cosine, sine, gains, queries, keys, values, lse, grads, kv_local
):
    rows_all = qkv.shape[0]
    groups = H // KV
    heads = kv_local * groups
    reach, rows = REACH, HALF
    q_width, k_width = heads * HD, kv_local * HD
    count = rows_all // reach
    block = lambda width: pl.BlockSpec((reach, width), lambda i: (count - 1 - i, 0))
    before = lambda width: pl.BlockSpec((reach, width), lambda i: (jnp.maximum(count - 2 - i, 0), 0))
    along = lambda height: pl.BlockSpec((height, reach), lambda i: (0, count - 1 - i))

    def kernel(
        qkv_ref, start_ref, cos_ref, sin_ref, gain_ref, q_ref, k_ref, k_before, v_ref, v_before,
        lse_ref, grad_ref, out_ref, gain_out, key_scr, value_scr, dq_scr, dk_scr, dv_scr,
    ):
        step = pl.program_id(0)
        blank = jnp.zeros((reach, k_width), F32)

        @pl.when(step == 0)
        def _():
            dk_scr[reach : 2 * reach, :] = blank
            dv_scr[reach : 2 * reach, :] = blank
            gain_out[...] = jnp.zeros_like(gain_out)

        @pl.when(step > 0)
        def _():
            dk_scr[reach : 2 * reach, :] = dk_scr[0:reach, :]
            dv_scr[reach : 2 * reach, :] = dv_scr[0:reach, :]

        dk_scr[0:reach, :] = blank
        dv_scr[0:reach, :] = blank
        key_scr[0:reach, :] = k_before[...]
        key_scr[reach : 2 * reach, :] = k_ref[...]
        value_scr[0:reach, :] = v_before[...]
        value_scr[reach : 2 * reach, :] = v_ref[...]
        for sub in range(0, reach, rows):
            allowed = window_mask(start_ref, count - 1 - step, sub, reach, rows)
            for kv in range(kv_local):
                lanes = slice(kv * HD, (kv + 1) * HD)
                span = slice(sub, sub + reach + rows)
                key = key_scr[span, lanes]
                value = value_scr[span, lanes]
                for head in range(kv * groups, (kv + 1) * groups):
                    head_lanes = slice(head * HD, (head + 1) * HD)
                    query = q_ref[sub : sub + rows, head_lanes]
                    grad = grad_ref[sub : sub + rows, head_lanes]
                    scores = jnp.where(allowed, dot_across(key, query, 1, 1), NEG_FILL)
                    probs = jnp.exp(scores - lse_ref[head : head + 1, sub : sub + rows])
                    grad_probs = dot_across(value, grad, 1, 1)
                    centre = row_sum(probs * grad_probs)
                    grad_scores = (probs * (grad_probs - centre)).astype(BF)
                    dq_scr[sub : sub + rows, head_lanes] = dot_across(grad_scores, key, 0, 0)
                    dk_scr[span, lanes] += product(grad_scores, query)
                    dv_scr[span, lanes] += product(probs.astype(BF), grad)

        cos, sin = cos_ref[...], sin_ref[...]

        def unturned(at, grad, gain):
            grad = grad * cos + pltpu.roll(grad * sin, HD // 2, 1)
            raw = qkv_ref[:, at : at + HD]
            inv = inverse_rms(raw)
            out_ref[:, at : at + HD] = norm_back(raw, inv, gain, grad).astype(BF)
            return row_sum(grad * raw * inv)

        sums = [jnp.zeros((1, HD), F32), jnp.zeros((1, HD), F32)]
        for head in range(heads):
            at = head * HD
            sums[0] += unturned(at, dq_scr[:, at : at + HD] * HD ** (-0.5), gain_ref[0:1, :])
        for head in range(kv_local):
            at = head * HD
            sums[1] += unturned(
                q_width + at, dk_scr[reach : 2 * reach, at : at + HD], gain_ref[1:2, :]
            )
            out_ref[:, q_width + k_width + at : q_width + k_width + at + HD] = dv_scr[
                reach : 2 * reach, at : at + HD
            ].astype(BF)
        gain_out[0:1, :] += sums[0]
        gain_out[1:2, :] += sums[1]

    return pl.pallas_call(
        kernel,
        grid=(count,),
        in_specs=[
            block(q_width + 2 * k_width),
            along(1),
            block(HD),
            block(HD),
            pl.BlockSpec((2, HD), lambda i: (0, 0)),
            block(q_width),
            block(k_width),
            before(k_width),
            block(k_width),
            before(k_width),
            along(heads),
            block(q_width),
        ],
        out_specs=[
            block(q_width + 2 * k_width),
            pl.BlockSpec((2, HD), lambda i: (0, 0)),
        ],
        out_shape=[
            jax.ShapeDtypeStruct((rows_all, q_width + 2 * k_width), BF),
            jax.ShapeDtypeStruct((2, HD), F32),
        ],
        scratch_shapes=[
            pltpu.VMEM((2 * reach, k_width), BF),
            pltpu.VMEM((2 * reach, k_width), BF),
            pltpu.VMEM((reach, q_width), F32),
            pltpu.VMEM((2 * reach, k_width), F32),
            pltpu.VMEM((2 * reach, k_width), F32),
        ],
        name="attention_backward",
    )(qkv, start, cosine, sine, gains, queries, keys, keys, values, values, lse, grads)


class Line:
    def __init__(self, axis):
        self.axis = axis
        self.place = lax.axis_index(axis)
        z = self.place
        near = jnp.where(z == 0, 1, z - 1)
        across = (z + 2) % 4
        last = jnp.where(z == 3, 0, jnp.where(z == 1, 2, 3))
        self.ids = (z, near, across, last)

    def send(self, block, pairs):
        return lax.ppermute(block, self.axis, pairs)

    def gather(self, block):
        z = self.place
        right = self.send(block, [(0, 1), (1, 2), (2, 3)])
        left = self.send(block, [(1, 0), (2, 1), (3, 2)])
        near = jnp.where(z == 0, left, right)
        right_two = self.send(right, [(1, 2), (2, 3)])
        left_two = self.send(left, [(1, 0), (2, 1)])
        across = jnp.where(z <= 1, left_two, right_two)
        far = self.send(across, [(1, 0), (2, 3)])
        last = jnp.where((z == 1) | (z == 2), left, far)
        return (block, near, across, last)

    def scatter(self, parts):
        own, near, across, last = parts
        z = self.place
        first = self.send(last().astype(BF), [(0, 1), (3, 2)])
        second = (first.astype(F32) + across()).astype(BF)
        right = self.send(second, [(0, 1), (1, 2)])
        left = self.send(second, [(3, 2), (2, 1)])
        near_part = near()
        right_out = (right.astype(F32) + jnp.where(z == 0, near_part, last())).astype(BF)
        left_out = (left.astype(F32) + near_part).astype(BF)
        right_in = self.send(right_out, [(0, 1), (1, 2), (2, 3)])
        left_in = self.send(left_out, [(1, 0), (2, 1), (3, 2)])
        return own() + (right_in.astype(F32) + left_in.astype(F32))


class Whole:
    def __init__(self, axis):
        self.axis = axis
        self.ids = (jnp.int32(0),)

    def gather(self, block):
        return (lax.all_gather(block, self.axis, axis=0, tiled=True),)

    def scatter(self, parts):
        return lax.psum_scatter(
            parts[0]().astype(BF), self.axis, scatter_dimension=0, tiled=True
        ).astype(F32)


def total_over(value, axes_sizes):
    for axis, size in axes_sizes:
        if size & (size - 1):
            value = lax.psum(value, axis)
            continue
        step = 1
        while step < size:
            value = value + lax.ppermute(value, axis, [(i, i ^ step) for i in range(size)])
            step *= 2
    return value


def build(sizes):
    tensor_size = sizes["tensor"]

    def per_device(
        tokens,
        segments,
        w_query,
        w_key,
        w_value,
        w_out,
        w_gate,
        w_up,
        w_down,
        attn_gain,
        mlp_gain,
        query_gain,
        key_gain,
        cotangent,
    ):
        seq_count, length = segments.shape
        rows_all = seq_count * length
        q_width = w_query.shape[1]
        k_width = w_key.shape[1]
        kv_local = k_width // HD
        hidden_width = w_gate.shape[1]
        line = Line("tensor") if tensor_size == 4 and seq_count == 1 else Whole("tensor")
        slot_count = len(line.ids)
        slot_rows = rows_all // slot_count
        starts = [ident * slot_rows for ident in line.ids]

        def in_order(blocks):
            if slot_count == 1:
                return blocks[0]
            result = jnp.zeros((rows_all,) + blocks[0].shape[1:], blocks[0].dtype)
            for start, block in zip(starts, blocks):
                result = lax.dynamic_update_slice_in_dim(result, block, start, 0)
            return result

        def in_slots(array):
            if slot_count == 1:
                return (array,)
            return tuple(lax.dynamic_slice_in_dim(array, start, slot_rows, 0) for start in starts)

        attn_w = lax.all_gather(
            jnp.concatenate([w_query, w_key, w_value, w_out.T], axis=1), "dp", axis=0, tiled=True
        )
        mlp_w = lax.all_gather(
            jnp.concatenate([w_gate, w_up, w_down.T], axis=1), "dp", axis=0, tiled=True
        )
        qkv_w = attn_w[:, : q_width + 2 * k_width]
        out_t = attn_w[:, q_width + 2 * k_width :]
        gate_up_w = mlp_w[:, : 2 * hidden_width]
        down_t = mlp_w[:, 2 * hidden_width :]

        inputs = tokens.astype(F32)
        inv_one = inverse_rms(inputs)
        normed_one = (inputs * inv_one * attn_gain).astype(BF)
        ones = line.gather(normed_one)
        qkv = in_order([product(block, qkv_w) for block in ones])

        places = positions(segments).reshape(-1)
        cosine, sine = rope_tables(places)
        start = (jnp.arange(rows_all, dtype=jnp.int32) - places)[None, :]
        head_gains = jnp.stack([query_gain, key_gain])
        query_low, key_low, values_low, attn_low, lse = attention_forward(
            qkv, start, cosine, sine, head_gains, kv_local
        )
        attn_slots = in_slots(attn_low)
        branch_one = line.scatter(
            [lambda block=block: product_back(block, out_t) for block in attn_slots]
        )
        middle = inputs + branch_one
        inv_two = inverse_rms(middle)
        normed_two = (middle * inv_two * mlp_gain).astype(BF)
        twos = line.gather(normed_two)
        tops = line.gather(cotangent)

        hiddens, gate_up_grads, lowered, middles = [], [], [], []
        for two, top in zip(twos, tops):
            gate_up = product(two, gate_up_w)
            grad_hidden = product(top, down_t)
            gate, up = gate_up[:, :hidden_width], gate_up[:, hidden_width:]
            sig = jax.nn.sigmoid(gate)
            silu = gate * sig
            hidden = (silu * up).astype(BF)
            gate_grad = (grad_hidden * up * sig * (1.0 + gate * (1.0 - sig))).astype(BF)
            up_grad = (grad_hidden * silu).astype(BF)
            gate_up_grad = jnp.concatenate([gate_grad, up_grad], axis=1)
            hiddens.append(hidden)
            gate_up_grads.append(gate_up_grad)
            middles.append(product_back(gate_up_grad, gate_up_w))
            lowered.append(product_back(hidden, down_t))
        grad_normed_two = line.scatter([lambda part=part: part for part in middles])
        branch_two = line.scatter([lambda part=part: part for part in lowered])
        output = middle + branch_two

        two_all = jnp.concatenate(twos, axis=0)
        top_all = jnp.concatenate(tops, axis=0)
        down_grad_t = product_over(top_all, jnp.concatenate(hiddens, axis=0)).astype(BF)
        gate_up_w_grad = product_over(two_all, jnp.concatenate(gate_up_grads, axis=0)).astype(BF)

        grad_mlp_gain = jnp.sum(grad_normed_two * middle * inv_two, axis=0)
        grad_middle = cotangent.astype(F32) + norm_back(
            middle, inv_two, mlp_gain, grad_normed_two
        )
        grad_mids = line.gather(grad_middle.astype(BF))
        grad_attn = in_order([product(block, out_t).astype(BF) for block in grad_mids])
        out_grad_t = product_over(
            jnp.concatenate(grad_mids, axis=0), jnp.concatenate(attn_slots, axis=0)
        ).astype(BF)

        qkv_grad, grad_head_gains = attention_backward(
            qkv, start, cosine, sine, head_gains, query_low, key_low, values_low, lse, grad_attn,
            kv_local,
        )
        qkv_grad_slots = in_slots(qkv_grad)
        grad_normed_one = line.scatter(
            [lambda block=block: product_back(block, qkv_w) for block in qkv_grad_slots]
        )
        qkv_w_grad = product_over(
            jnp.concatenate(ones, axis=0), jnp.concatenate(qkv_grad_slots, axis=0)
        ).astype(BF)
        grad_attn_gain = jnp.sum(grad_normed_one * inputs * inv_one, axis=0)
        tokens_grad = grad_middle + norm_back(inputs, inv_one, attn_gain, grad_normed_one)

        def shard(grad):
            return lax.psum_scatter(grad, "dp", scatter_dimension=0, tiled=True).astype(F32)

        down_shard = shard(down_grad_t).T
        gate_up_shard = shard(gate_up_w_grad)
        out_shard = shard(out_grad_t).T
        qkv_shard = shard(qkv_w_grad)

        gains = jnp.concatenate([grad_attn_gain, grad_mlp_gain, grad_head_gains.reshape(-1)])
        gains = total_over(gains, [("dp", sizes["dp"]), ("tensor", tensor_size)])
        width = attn_gain.shape[0]
        return (
            output,
            tokens_grad,
            qkv_shard[:, :q_width],
            qkv_shard[:, q_width : q_width + k_width],
            qkv_shard[:, q_width + k_width :],
            out_shard,
            gate_up_shard[:, :hidden_width],
            gate_up_shard[:, hidden_width:],
            down_shard,
            gains[:width],
            gains[width : 2 * width],
            gains[2 * width : 2 * width + HD],
            gains[2 * width + HD :],
        )

    return per_device


def solution(mesh):
    rows = P(("dp", "tensor"), None)
    split = P("dp", "tensor")
    turned = P("tensor", "dp")
    return jax.shard_map(
        build(dict(mesh.shape)),
        mesh=mesh,
        in_specs=(
            rows,
            P("dp", None),
            split,
            split,
            split,
            turned,
            split,
            split,
            turned,
            P(),
            P(),
            P(),
            P(),
            rows,
        ),
        out_specs=(
            rows,
            rows,
            split,
            split,
            split,
            turned,
            split,
            split,
            turned,
            P(),
            P(),
            P(),
            P(),
        ),
        check_vma=False,
    )
```
